32 devices in a mesh: row: 4 (over y, x), col: 4 (over z), dp: 2 (over core).
Axes of the slice: x: 2, y: 2, z: 4, core: 2. Of those that a mesh axis runs over, the one named last changes fastest.
Arguments:
- audio_embed: bfloat16 [4096, 8192], P('dp', 'row'), may hold values from -400 to 400
- video_embed: bfloat16 [4096, 8192], P('dp', 'col'), may hold values from -500 to 500
- video_hidden: bfloat16 [4096, 8192], P('dp', 'row'), may hold values from -6 to 6
Outputs:
- weight_grad: float32 [8192, 8192], P(('row', 'dp'), 'col')
The draws below stay inside these ranges and needn't reach their ends.
All inputs are finite; a program needn't handle non-finite values.
Results may differ from the reference program's by a relative error of at most 0.0056.
Values may be sent and summed in bfloat16 or wider, within the bound.
No kernel may reach another device: no remote copies, remote signals or barrier semaphores. Data moves between devices by JAX's collectives and lax.ppermute only.
A program may use at most 128 MiB of HBM per device.

```python
import math
import jax
import jax.numpy as jnp
from jax import lax

F = 8192
H = 8192
ROWS_DP = 2048
B = 4096
N_DP = 2


def paired_embeds(key):
    keys = [jax.random.fold_in(key, 7100 + offset) for offset in range(8)]
    shape = (B, F)
    common = jnp.clip(jax.random.normal(keys[0], shape, jnp.float32), -4.0, 4.0)
    private = jnp.clip(jax.random.normal(keys[1], shape, jnp.float32), -4.0, 4.0)
    position = (jnp.arange(B) % ROWS_DP).astype(jnp.float32)
    ramp = 1.0 + 2.0 * position / ROWS_DP
    row_scale = (jnp.exp(jax.random.uniform(keys[2], (B,), jnp.float32, 0.0, math.log(10.0))) * ramp)[:, None]
    audio_gain = jnp.exp(jax.random.uniform(keys[3], (1, F), jnp.float32, math.log(0.3), math.log(3.0)))
    video_gain = jnp.exp(jax.random.uniform(keys[4], (1, F), jnp.float32, math.log(0.3), math.log(3.0)))
    audio_shift = jax.random.uniform(keys[5], (1, F), jnp.float32, -1.0, 1.0)
    video_shift = jax.random.uniform(keys[6], (1, F), jnp.float32, -1.0, 1.0)
    mismatch = jnp.exp(jax.random.uniform(keys[7], (1, F), jnp.float32, math.log(0.001), math.log(0.1)))
    audio = audio_shift + audio_gain * row_scale * common
    video = video_shift + video_gain * row_scale * (jnp.sqrt(1.0 - mismatch) * common + jnp.sqrt(mismatch) * private)
    return (audio, video)


def draw_audio_embed(key, part):
    return paired_embeds(key)[0].astype(jnp.bfloat16)


def draw_video_embed(key, part):
    return paired_embeds(key)[1].astype(jnp.bfloat16)


def levels(stream_key, extent, pieces, low, high):
    gain, own = 1.0, jax.random.fold_in(stream_key, 6)
    for dim, blocks in pieces:
        draws = jnp.exp(jax.random.uniform(jax.random.fold_in(own, dim), (blocks,), jnp.float32, low / len(pieces), high / len(pieces)))
        gain = gain * jnp.repeat(draws, extent[dim] // blocks).reshape([-1 if axis == dim else 1 for axis in range(len(extent))])
    return gain


def scatter_about(key, extent, spread, most, pieces=(), held_as=jnp.bfloat16):
    result = spread * jax.random.normal(key, extent, jnp.float32)
    if pieces:
        result = result * levels(key, extent, pieces, -0.22, 0.18)
    return jnp.clip(result, -most, most).astype(held_as)


def setup_inputs(seed: int = 0) -> dict:
    key_of = jax.random.split(jax.random.key(seed), 4)
    audio_embed = draw_audio_embed(jax.random.fold_in(key_of[3], 71), 0)
    video_embed = draw_video_embed(jax.random.fold_in(key_of[3], 71), 0)
    video_hidden = scatter_about(key_of[2], (B, H), 1.0, 6.0, ((0, 2), (1, 4)))
    return {"audio_embed": audio_embed, "video_embed": video_embed, "video_hidden": video_hidden}


off_weight = 0.0051
loss_scale = 8192.0
epsilon = 1e-05

def standardize(values):
    grouped = values.astype(jnp.float32).reshape(N_DP, ROWS_DP, values.shape[1])
    center = lax.optimization_barrier(jnp.mean(grouped, axis=1, keepdims=True))
    second = lax.optimization_barrier(jnp.mean(grouped * grouped, axis=1, keepdims=True))
    inv_scale = lax.rsqrt(second - center * center + epsilon)
    normed = ((grouped - center) * inv_scale).astype(jnp.bfloat16)
    return (normed.reshape(values.shape), inv_scale)

def reference(audio_embed, video_embed, video_hidden):
    contract = (((0,), (0,)), ((), ()))
    audio_norm = standardize(audio_embed)[0]
    video_norm, video_inv = standardize(video_embed)
    correlation = lax.dot_general(audio_norm, video_norm, contract, preferred_element_type=jnp.float32) / B
    diagonal_mask = jnp.arange(F)[:, None] == jnp.arange(F)[None, :]
    grad_corr = jnp.where(diagonal_mask, -2.0 * (1.0 - correlation), 2.0 * off_weight * correlation).astype(jnp.bfloat16)
    grad_norm = jnp.dot(audio_norm, grad_corr, preferred_element_type=jnp.float32) * (loss_scale / B)
    grouped = grad_norm.reshape(N_DP, ROWS_DP, F)
    video_group = video_norm.astype(jnp.float32).reshape(N_DP, ROWS_DP, F)
    bn_term = lax.optimization_barrier(jnp.mean(grouped * video_group, axis=1, keepdims=True))
    grad_video = ((grouped - video_group * bn_term) * video_inv).astype(jnp.bfloat16).reshape(B, F)
    return lax.dot_general(video_hidden, grad_video, contract, preferred_element_type=jnp.float32)
```

```python
import jax
import jax.numpy as jnp
from jax import lax
from jax.sharding import PartitionSpec as P

off_weight = 0.0051
loss_scale = 8192.0
epsilon = 1e-05


def statistics(values):
    floats = values.astype(jnp.float32)
    center = jnp.sum(floats, axis=0) / values.shape[0]
    second = jnp.sum(floats * floats, axis=0) / values.shape[0]
    return center, lax.rsqrt(second - center * center + epsilon)


def normalize(values, center, inv_scale):
    return ((values.astype(jnp.float32) - center) * inv_scale).astype(jnp.bfloat16)


def contract_rows(left, right):
    return lax.dot_general(
        left, right, (((0,), (0,)), ((), ())), preferred_element_type=jnp.float32
    )


def product(left, right):
    return jnp.dot(left, right, preferred_element_type=jnp.float32)


def swap(values, axis, bit):
    count = lax.axis_size(axis)
    return lax.ppermute(values, axis, [(i, i ^ (1 << bit)) for i in range(count)])


class Halving:
    def __init__(self, bits, rows):
        self.bits = bits
        me = lax.axis_index("row")
        start, length = 0, rows
        self.sent = []
        self.lengths = []
        for bit in bits:
            length //= 2
            mine = (me >> bit) & 1
            self.sent.append(start + (1 - mine) * length)
            self.lengths.append(length)
            start = start + mine * length
        self.start, self.length = start, length

    def pieces(self, values):
        take = lax.dynamic_slice_in_dim
        parts = [take(values, s, l, 0) for s, l in zip(self.sent, self.lengths)]
        return parts, take(values, self.start, self.length, 0)

    def gather_order(self, values):
        sent, own = self.pieces(values)
        return own, sent


def on_device(audio_embed, video_embed, video_hidden):
    local_rows = audio_embed.shape[0]
    n_dp = lax.axis_size("dp")
    total_rows = local_rows * n_dp
    width_audio = audio_embed.shape[1]
    width_video = video_embed.shape[1]
    row_parts = lax.axis_size("row")
    n_bits = row_parts.bit_length() - 1
    assert row_parts == 1 << n_bits and n_dp == 2
    scaled = loss_scale / total_rows

    chunks = max(1, width_video // 512)
    width = width_video // chunks
    half = width // 2

    audio_stats = statistics(audio_embed)
    audio_norm = normalize(audio_embed, *audio_stats)
    orders = [
        Halving(list(range(n_bits)), local_rows),
        Halving(list(range(n_bits))[::-1], local_rows),
    ]
    audio_parts = [
        jax.tree.map(lambda x: normalize(x, *audio_stats), o.pieces(audio_embed)) for o in orders
    ]
    first_audio = lax.axis_index("row") * width_audio + jnp.arange(width_audio, dtype=jnp.int32)
    own_half = lax.axis_index("dp")
    half_hidden = video_hidden.shape[1] // 2

    def gather_order(order, values):
        me = lax.axis_index("row")
        offsets = []
        for index in range(row_parts):
            other = me
            for stage in range(n_bits):
                if (index >> stage) & 1:
                    other = other ^ (1 << order.bits[n_bits - 1 - stage])
            start = 0
            length = local_rows
            for bit in order.bits:
                length //= 2
                start = start + ((other >> bit) & 1) * length
            offsets.append(start)
        return jnp.concatenate(
            [lax.dynamic_slice_in_dim(values, s, order.length, 0) for s in offsets]
        )

    hidden = [gather_order(o, video_hidden) for o in orders]
    outs = []
    for chunk in range(chunks):
        video = video_embed[:, chunk * width : (chunk + 1) * width]
        center, inv = statistics(video)
        video_norm = normalize(video, center, inv)
        own_corr = contract_rows(audio_norm, video_norm)
        corr = (own_corr + swap(own_corr, "dp", 0)) / total_rows
        first_video = (
            lax.axis_index("col") * width_video
            + chunk * width
            + jnp.arange(width, dtype=jnp.int32)
        )
        diagonal = first_audio[:, None] == first_video[None, :]
        grad_corr = jnp.where(
            diagonal, -2.0 * (1.0 - corr), 2.0 * off_weight * corr
        ).astype(jnp.bfloat16)
        bn_term = jnp.sum(grad_corr.astype(jnp.float32) * own_corr, axis=0)
        for bit in range(n_bits):
            bn_term = bn_term + swap(bn_term, "row", bit)
        bn_term = bn_term * (scaled / local_rows)
        for side, order in enumerate(orders):
            cols = slice(side * half, (side + 1) * half)
            right = grad_corr[:, cols]
            sends, keep = audio_parts[side]
            received = None
            for stage, bit in enumerate(order.bits):
                term = product(sends[stage], right)
                for got_start, got in received or []:
                    length = order.lengths[stage]
                    mine = (lax.axis_index("row") >> bit) & 1
                    term = term + lax.dynamic_slice_in_dim(
                        got, (1 - mine) * length, length, 0
                    ).astype(jnp.float32)
                got = swap(term.astype(jnp.bfloat16), "row", bit)
                new = []
                for _, old in received or []:
                    mine = (lax.axis_index("row") >> bit) & 1
                    new.append((0, lax.dynamic_slice_in_dim(old, mine * order.lengths[stage], order.lengths[stage], 0)))
                received = new + [(0, got)]
            slab = product(keep, right)
            for _, got in received or []:
                slab = slab + got.astype(jnp.float32)
            slab = slab * scaled
            own_video = normalize(
                lax.dynamic_slice_in_dim(video[:, cols], order.start, order.length, 0),
                center[cols],
                inv[cols],
            ).astype(jnp.float32)
            grad = ((slab - own_video * bn_term[cols]) * inv[cols]).astype(jnp.bfloat16)
            for bit in order.bits[::-1]:
                grad = jnp.concatenate([grad, swap(grad, "row", bit)])
            left = hidden[side]
            other = lax.dynamic_slice_in_dim(left, (1 - own_half) * half_hidden, half_hidden, 1)
            mine = lax.dynamic_slice_in_dim(left, own_half * half_hidden, half_hidden, 1)
            got = swap(contract_rows(other, grad), "dp", 0)
            outs.append(contract_rows(mine, grad) + got)
    return jnp.concatenate(outs, axis=1)


def solution(mesh):
    return jax.shard_map(
        on_device,
        mesh=mesh,
        in_specs=(P("dp", "row"), P("dp", "col"), P("dp", "row")),
        out_specs=P(("row", "dp"), "col"),
        check_vma=False,
    )
```
